512 devices in a mesh: grp: 16 (over x, z_lo, core), blk: 32 (over z_hi, y).
Axes of the slice: x: 4, y: 8, z: 8 (z_hi: 4, z_lo: 2; z = z_hi * 2 + z_lo), core: 2. Of those that a mesh axis runs over, the one named last changes fastest.
Arguments:
- particles: bfloat16 [1024, 2, 4000], P(('blk', 'grp')), may hold values from -6 to 6
- ctf_class: int32 [1024], P(('blk', 'grp')), may hold values from 0 to 63
- orient_prior: bfloat16 [1024, 192], P(('blk', 'grp')), may hold values from -6 to 6
- ctf_curves: float32 [64, 4000], replicated, may hold values from -1 to 1
- noise_weight: float32 [4000], replicated, may hold values from 0.005 to 0.05
- shift_phase: float32 [9, 4000], replicated, may hold values from -3.140625 to 3.140625
- trans_index: int32 [9], replicated, may hold values from 0 to 8, each once
- projections: bfloat16 [4096, 2, 4000], P(('grp', 'blk')), may hold values from -1.75 to 1.75
- orient_subset: int32 [4096], P(('grp', 'blk')), may hold values from 0 to 191
Outputs:
- scores: float32 [1024, 9, 4096], P('blk', None, 'grp')
The draws below stay inside these ranges and needn't reach their ends.
Inputs may be any that keep to these rules, and one draw needn't show every extreme that they name: `trans_index`: each row of shift_phase is named once.
All inputs are finite; a program needn't handle non-finite values.
Results may differ from the reference program's by a relative error of at most 0.00056.
Values may be sent and summed in bfloat16 or wider, within the bound.
A program may use at most 128 MiB of HBM per device.

```python
import math
import jax
import jax.numpy as jnp
from jax import lax

K = 4000
NT = 9
NC = 64
SUBSETS = 192
PROJ_DEV = 8
NPART = 1024
NPROJ = 4096
N_BLK = 32


def plant(values, stream_key, smallest, high):
    longest = values.shape.index(max(values.shape))
    spots = []
    for shift in (0, 1):
        where = [jax.random.randint(jax.random.fold_in(stream_key, axis), (), 0, length) for axis, length in enumerate(values.shape)]
        where[longest] = (where[longest] + shift) % values.shape[longest]
        spots.append(tuple(where))
    return values.at[spots[0]].set(smallest).at[spots[1]].set(high)


def steps_of(own_key, dims, split, least, high):
    level = 1.0
    for dim, parts in split:
        draws = jax.random.uniform(jax.random.fold_in(jax.random.fold_in(own_key, 6), dim), (parts,), jnp.float32, least / len(split), high / len(split))
        level = level * jnp.repeat(jnp.exp(draws), dims[dim] // parts).reshape((-1,) + (1,) * (len(dims) - 1 - dim))
    return level


def noise(key, extent, spread, bound, pieces=(), held_as=jnp.bfloat16):
    values = jax.random.normal(key, extent, jnp.float32) * spread
    if len(pieces) > 0:
        values = steps_of(key, extent, pieces, -0.22, 0.18) * values
    return jnp.clip(values, min=-bound, max=bound).astype(held_as)


def setup_inputs(seed: int = 0) -> dict:
    arg_keys = jax.random.split(jax.random.key(seed), 10)
    particles = noise(arg_keys[0], (NPART, 2, K), 1.0, 6.0, ((0, 512),))
    ctf_class = plant(jax.random.randint(arg_keys[1], (NPART,), 0, NC), jax.random.fold_in(arg_keys[1], 1), 0, NC - 1).astype(jnp.int32)
    orient_prior = noise(arg_keys[2], (NPART, SUBSETS), 1.0, 6.0, ((0, 512),))
    ctf_curves = jnp.clip(jax.random.uniform(arg_keys[3], (NC, K), jnp.float32, -1.0, 1.0), -1.0, 1.0)
    noise_weight = jnp.clip(jnp.exp(jax.random.uniform(arg_keys[4], (K,), jnp.float32, math.log(0.005), math.log(0.05))), 0.005, 0.05)
    shift_phase = jnp.clip(jax.random.uniform(arg_keys[5], (NT, K), jnp.float32, -3.140625, 3.140625), -3.140625, 3.140625)
    trans_index = jax.random.permutation(arg_keys[6], NT).astype(jnp.int32)
    projections = noise(arg_keys[7], (NPROJ, 2, K), 0.3, 1.75, ((0, 512),))
    orient_subset = plant(jax.random.randint(arg_keys[8], (NPROJ,), 0, SUBSETS), jax.random.fold_in(arg_keys[8], 1), 0, SUBSETS - 1).astype(jnp.int32)
    return {"particles": particles, "ctf_class": ctf_class, "orient_prior": orient_prior, "ctf_curves": ctf_curves, "noise_weight": noise_weight, "shift_phase": shift_phase, "trans_index": trans_index, "projections": projections, "orient_subset": orient_subset}


def reference(particles, ctf_class, orient_prior, ctf_curves, noise_weight, shift_phase, trans_index, projections, orient_subset):
    highest = lax.Precision.HIGHEST
    weight_rows = ctf_curves * noise_weight[None, :]
    curve = weight_rows[ctf_class]
    weighted = (particles.astype(jnp.float32) * curve[:, None, :]).astype(jnp.bfloat16)
    weighted_wide = weighted.astype(jnp.float32)
    angle = shift_phase[trans_index]
    cos_part = jnp.cos(angle)
    sin_part = jnp.sin(angle)
    curve_sq = ctf_curves * ctf_curves * noise_weight[None, :]
    prior = orient_prior.astype(jnp.float32)
    block_len = PROJ_DEV * N_BLK
    blocks = NPROJ // block_len
    bank_blocks = projections.reshape(blocks, block_len, 2, K)
    id_blocks = orient_subset.reshape(blocks, block_len)

    def score_block(inputs):
        bank, subset_ids = inputs
        bank_real = bank[:, 0, :].astype(jnp.float32)
        bank_imag = bank[:, 1, :].astype(jnp.float32)
        real_shift = cos_part[:, None, :] * bank_real[None] + sin_part[:, None, :] * bank_imag[None]
        imag_shift = cos_part[:, None, :] * bank_imag[None] - sin_part[:, None, :] * bank_real[None]
        shifted = jnp.stack([real_shift, imag_shift], axis=2).astype(jnp.bfloat16)
        cross = jnp.einsum("nck,tmck->ntm", weighted_wide, shifted.astype(jnp.float32), precision=highest)
        power = bank_real * bank_real + bank_imag * bank_imag
        norm_table = jnp.dot(curve_sq, power.T, precision=highest)
        norm_sel = norm_table[ctf_class]
        prior_term = prior[:, subset_ids]
        return cross - 0.5 * norm_sel[:, None, :] + prior_term[:, None, :]

    result = lax.map(score_block, (bank_blocks, id_blocks))
    return jnp.transpose(result, (1, 2, 0, 3)).reshape(NPART, NT, NPROJ)
```

```python
import functools

import jax
import jax.numpy as jnp
from jax import lax
from jax.experimental import pallas as pl
from jax.experimental.pallas import tpu as pltpu
from jax.sharding import PartitionSpec as P

MESH = pl.DeviceIdType.MESH
NX, NZL, NC, NZH, NY = 4, 2, 2, 4, 8
NZ = NZH * NZL
NT = 9
PJ = 8
LANES = 128
KE = 33 * LANES
KH = 17 * LANES
PIECES = ((0, 8), (8, 8), (16, 8), (24, 9))
NJ = NY * PJ
NS = (NT * NJ + LANES - 1) // LANES
ROWS = NZ * NX * 8


def rem(a, n):
    return lax.rem(a, jnp.int32(n))


def div(a, n):
    return lax.div(a, jnp.int32(n))


def kernel(
    pc, wc, cosr, sinr, out,
    bank, wrecv, wbuf, sbuf, acc0, acc1, ebuf, rbuf,
    lsem, ysend, yrecv, zsend, zrecv, xsend, xrecv, psend, precv, csend, crecv, esend, erecv,
):
    grp = lax.axis_index("grp")
    blk = lax.axis_index("blk")
    x, zl, core = div(grp, 4), rem(div(grp, 2), 2), rem(grp, 2)
    zh, y = div(blk, 8), rem(blk, 8)
    z = zh * 2 + zl

    def dev(x_=x, z_=z, core_=core, y_=y):
        return ((x_ * 2 + rem(z_, 2)) * 2 + core_, div(z_, 2) * 8 + y_)

    partner = dev(core_=1 - core)
    yr, yl = dev(y_=rem(y + 1, NY)), dev(y_=rem(y + NY - 1, NY))
    zr, zlft = dev(z_=rem(z + 1, NZ)), dev(z_=rem(z + NZ - 1, NZ))
    xp = [dev(x_=rem(x + d, NX)) for d in (1, 2, 3)]
    ep = [dev(z_=rem(z + 2 * d, NZ)) for d in (1, 2, 3)]

    barrier = pltpu.get_barrier_semaphore()
    peers = [partner, yr, yl, zr, zlft] + xp + ep
    for p in peers:
        pl.semaphore_signal(barrier, inc=1, device_id=p, device_id_type=MESH)
    pl.semaphore_wait(barrier, len(peers))

    started = []

    def send(src, dst, ss, rs, to):
        c = pltpu.make_async_remote_copy(
            src_ref=src, dst_ref=dst, send_sem=ss, recv_sem=rs, device_id=to, device_id_type=MESH
        )
        c.start()
        started.append(c)

    def arrive(dst, ss, rs, frm):
        pltpu.make_async_remote_copy(
            src_ref=dst, dst_ref=dst, send_sem=ss, recv_sem=rs, device_id=frm, device_id_type=MESH
        ).wait_recv()

    def lanes(q):
        return pl.ds(PIECES[q][0] * LANES, PIECES[q][1] * LANES)

    def in_step(s, d, q):
        return s < 4 or (q < 2) == (d == 0)

    def y_send(s, q):
        for d, to in ((0, yr), (1, yl)):
            if in_step(s, d, q):
                y_send1(s, q, d, to)

    def y_send1(s, q, d, to):
        o = rem(y + (NY - (s - 1) if d == 0 else s - 1), NY)
        src = pc.at[:, lanes(q)] if s == 1 else bank.at[o, :, lanes(q)]
        send(src, bank.at[o, :, lanes(q)], ysend.at[d, s - 1, q], yrecv.at[d, s - 1, q], to)

    def y_step(s):
        for q in range(4):
            for d, to in ((0, yr), (1, yl)):
                if in_step(s, d, q):
                    o = rem(y + (NY - s if d == 0 else s), NY)
                    arrive(bank.at[o, :, lanes(q)], ysend.at[d, s - 1, q], yrecv.at[d, s - 1, q], to)
                    if s < 4 and in_step(s + 1, d, q):
                        y_send1(s + 1, q, d, to)

    def wblock(o, h=None):
        xs = slice(None) if h is None else pl.ds(2 * h, 2)
        return (div(o, 2), xs, rem(o, 2))

    def z_send(s, d):
        o = rem(z + (NZ - (s - 1) if d == 0 else s - 1), NZ)
        a, b, c = wblock(o, d if s == 4 else None)
        ref = wbuf.at[core, a, b, c]
        send(ref, ref, zsend.at[d, s - 1], zrecv.at[d, s - 1], zr if d == 0 else zlft)

    def p_send(s, d, o):
        a, b, c = wblock(o, d if s == 4 else None)
        ref = wbuf.at[core, a, b, c]
        send(ref, ref, psend.at[d, s], precv.at[d, s], partner)

    def p_wait(s, d, o):
        a, b, c = wblock(o, d if s == 4 else None)
        arrive(wbuf.at[1 - core, a, b, c], psend.at[d, s], precv.at[d, s], partner)

    def z_origin(s, d):
        return rem(z + (NZ - s if d == 0 else s), NZ)

    def z_step(s):
        for d in (0, 1):
            o = z_origin(s, d)
            a, b, c = wblock(o, d if s == 4 else None)
            arrive(wbuf.at[core, a, b, c], zsend.at[d, s - 1], zrecv.at[d, s - 1], zr)
            if s < 4:
                z_send(s + 1, d)
            p_send(s, d, o)

    def shift_tiles(first, count):
        def body(i, carry):
            at = pl.ds(pl.multiple_of(i * LANES, LANES), LANES)
            real, imag = [], []
            for yy in range(NY):
                both = bank[yy, :, at].astype(jnp.float32)
                real.append(both[:PJ])
                imag.append(both[PJ:])
            for t in range(NT):
                c = jnp.broadcast_to(cosr[pl.ds(t, 1), at], (PJ, LANES))
                s = jnp.broadcast_to(sinr[pl.ds(t, 1), at], (PJ, LANES))
                for m in range(0, NY, 2):
                    r0 = c * real[m] + s * imag[m]
                    r1 = c * real[m + 1] + s * imag[m + 1]
                    i0 = c * imag[m] - s * real[m]
                    i1 = c * imag[m + 1] - s * real[m + 1]
                    rows = pl.ds(t * NJ + m * PJ, 2 * PJ)
                    sbuf[0, rows, at] = jnp.concatenate([r0, r1], axis=0).astype(jnp.bfloat16)
                    sbuf[1, rows, at] = jnp.concatenate([i0, i1], axis=0).astype(jnp.bfloat16)
            return carry

        lax.fori_loop(first, first + count, body, 0)

    local = pltpu.make_async_copy(pc, bank.at[y], lsem)
    local.start()
    send(wc.at[1 - core], wrecv, csend, crecv, partner)
    for q in range(4):
        y_send(1, q)
    arrive(wrecv, csend, crecv, partner)
    mine = wc[core].astype(jnp.float32)
    theirs = wrecv[...].astype(jnp.float32)
    first = jnp.where(core == 0, mine, theirs)
    second = jnp.where(core == 0, theirs, mine)
    wbuf[core, zh, x, zl] = jnp.concatenate([first, second], axis=0).astype(jnp.bfloat16)
    own = wbuf.at[core, zh, x, zl]
    for d in range(3):
        send(own, own, xsend.at[d], xrecv.at[d], xp[d])
    y_step(1)
    for d in range(3):
        arrive(wbuf.at[core, zh, rem(x + NX - 1 - d, NX), zl], xsend.at[d], xrecv.at[d], xp[d])
    z_send(1, 0)
    z_send(1, 1)
    p_send(0, 0, z)
    y_step(2)
    z_step(1)
    y_step(3)
    z_step(2)
    y_step(4)
    local.wait()
    shift_tiles(0, 16)
    z_step(3)
    shift_tiles(16, 17)
    z_step(4)
    p_wait(0, 0, z)
    for s in range(1, 5):
        for d in (0, 1):
            p_wait(s, d, z_origin(s, d))

    dims = (((1,), (1,)), ((), ()))
    for part, acc in ((0, acc0), (1, acc1)):
        fresh = True
        for kh, lo, n, base in ((0, 0, 8, 0), (0, 8, 8, 0), (1, 0, 8, 16), (1, 8, 9, 16)):
            w = wbuf[kh, :, :, :, :, pl.ds(lo * LANES, n * LANES)].reshape(ROWS, n * LANES)
            sh = sbuf[part, :, pl.ds((base + lo) * LANES, n * LANES)]
            prod = lax.dot_general(w, sh, dims, preferred_element_type=jnp.float32)
            tail = jnp.zeros((ROWS, NS * LANES - NT * NJ), jnp.float32)
            prod = jnp.concatenate([prod, tail], axis=1)
            for n in range(NS):
                slab = prod[:, n * LANES : (n + 1) * LANES]
                acc[n] = slab if fresh else acc[n] + slab
            fresh = False

    for d in (2, 1, 3, 0):
        o = rem(zh + d, NZH)
        for n in range(NS):
            val = acc0[n, pl.ds(o * 64, 32, stride=2), :] + acc1[n, pl.ds(o * 64 + 1, 32, stride=2), :]
            if d == 0:
                rbuf[zh, n] = val
            else:
                ebuf[d - 1, n] = val
        if d:
            send(ebuf.at[d - 1], rbuf.at[zh], esend.at[d - 1], erecv.at[d - 1], ep[d - 1])
    for d in (1, 3, 2):
        arrive(rbuf.at[rem(zh + NZH - d, NZH)], esend.at[d - 1], erecv.at[d - 1], ep[d - 1])
    for t in range(NT):
        slab, col = t // 2, pl.ds(t % 2 * NJ, NJ)
        for m in range(0, NZH, 2):
            out[t, :, pl.ds(m * NJ, 2 * NJ)] = jnp.concatenate(
                [rbuf[m, slab, :, col], rbuf[m + 1, slab, :, col]], axis=1
            )
    for c in started:
        c.wait_send()


def split3(v):
    hi = lax.reduce_precision(v, 8, 7)
    mid = lax.reduce_precision(v - hi, 8, 7)
    lo = v - hi - mid
    return hi.astype(jnp.bfloat16), mid.astype(jnp.bfloat16), lo.astype(jnp.bfloat16)


def per_device(
    particles,
    ctf_class,
    orient_prior,
    ctf_curves,
    noise_weight,
    shift_phase,
    trans_index,
    projections,
    orient_subset,
):
    highest = lax.Precision.HIGHEST
    bf16 = jnp.bfloat16
    nclass = ctf_curves.shape[0]
    nsub = orient_prior.shape[1]
    k = ctf_curves.shape[1]
    half = nsub // 2

    def onehot(ids, n, dtype):
        return (ids[:, None] == jnp.arange(n, dtype=jnp.int32)[None, :]).astype(dtype)

    weight_rows = ctf_curves * noise_weight[None, :]
    curve_sq = weight_rows * ctf_curves
    hot = onehot(ctf_class, nclass, jnp.float32)
    curve = jnp.dot(hot, weight_rows, precision=highest)
    weighted = (particles.astype(jnp.float32) * curve[:, None, :]).astype(bf16)
    hotb = hot.astype(bf16)
    none = jnp.zeros_like(hotb)
    wext = jnp.stack(
        [
            jnp.concatenate([orient_prior[:, :half], hotb, hotb], axis=1),
            jnp.concatenate([orient_prior[:, half:], hotb, none], axis=1),
        ],
        axis=1,
    )
    wfull = jnp.concatenate([weighted, wext], axis=2).reshape(4, KE)
    wc = jnp.stack([wfull[:, :KH], wfull[:, KE - KH :]], axis=0)

    real = projections[:, 0, :].astype(jnp.float32)
    imag = projections[:, 1, :].astype(jnp.float32)
    power = real * real + imag * imag
    norm = -0.5 * lax.dot_general(power, curve_sq, (((1,), (1,)), ((), ())), precision=highest)
    hi, mid, lo = split3(norm)
    sub = onehot(orient_subset, nsub, bf16)
    pext = jnp.concatenate(
        [
            jnp.concatenate([sub[:, :half], hi, mid], axis=1),
            jnp.concatenate([sub[:, half:], lo, jnp.zeros_like(lo)], axis=1),
        ],
        axis=0,
    )
    pc = jnp.concatenate(
        [jnp.concatenate([projections[:, 0, :], projections[:, 1, :]], axis=0), pext], axis=1
    )

    pick = onehot(trans_index, shift_phase.shape[0], jnp.float32)
    angle = jnp.dot(pick, shift_phase, precision=highest)
    angle = jnp.pad(angle, ((0, 0), (0, KE - k)))
    cosr, sinr = jnp.cos(angle), jnp.sin(angle)

    dma = pltpu.SemaphoreType.DMA
    vm = pl.BlockSpec(memory_space=pltpu.VMEM)
    scores = pl.pallas_call(
        kernel,
        out_shape=jax.ShapeDtypeStruct((NT, 32, NZH * NJ), jnp.float32),
        in_specs=[vm] * 4,
        out_specs=vm,
        scratch_shapes=[
            pltpu.VMEM((NY, 2 * PJ, KE), bf16),
            pltpu.VMEM((4, KH), bf16),
            pltpu.VMEM((2, NZH, NX, NZL, 8, KH), bf16),
            pltpu.VMEM((2, NT * NJ, KE), bf16),
            pltpu.VMEM((NS, ROWS, LANES), jnp.float32),
            pltpu.VMEM((NS, ROWS, LANES), jnp.float32),
            pltpu.VMEM((3, NS, 32, LANES), jnp.float32),
            pltpu.VMEM((NZH, NS, 32, LANES), jnp.float32),
            dma,
            dma((2, 4, 4)),
            dma((2, 4, 4)),
            dma((2, 4)),
            dma((2, 4)),
            dma((3,)),
            dma((3,)),
            dma((2, 5)),
            dma((2, 5)),
            dma,
            dma,
            dma((3,)),
            dma((3,)),
        ],
        compiler_params=pltpu.CompilerParams(
            collective_id=0, has_side_effects=True, vmem_limit_bytes=48 << 20
        ),
        name="scores",
    )(pc, wc, cosr, sinr)
    return jnp.transpose(scores, (1, 0, 2))


def solution(mesh):
    placed = (
        P(("blk", "grp"), None, None),
        P(("blk", "grp")),
        P(("blk", "grp"), None),
        P(),
        P(),
        P(),
        P(),
        P(("grp", "blk"), None, None),
        P(("grp", "blk")),
    )
    return jax.shard_map(
        per_device, mesh=mesh, in_specs=placed, out_specs=P("blk", None, "grp"), check_vma=False
    )
```

```python
import jax
import jax.numpy as jnp
from jax import lax
from jax.experimental import pallas as pl
from jax.experimental.pallas import tpu as pltpu
from jax.sharding import PartitionSpec as P

MESH = pl.DeviceIdType.MESH
NX, NZL, NC, NZH, NY = 4, 2, 2, 4, 8
NZ = NZH * NZL
NT = 9
PJ = 8
LANES = 128
KE = 33 * LANES
KH = 17 * LANES
MAIN = 31
PIECES = ((0, 10), (10, 10), (20, 11), (31, 2))
NQ = len(PIECES)
NJ = NY * PJ
NS = 5
NJ = NY * PJ
EARLY, LATE = (7, 0, 1), (2, 3, 4, 5, 6)
GROUPS = ((EARLY, 0, 2), (LATE, 2, 3))
ROWS = NZ * NX * 8


def rem(a, n):
    return lax.rem(a, jnp.int32(n))


def div(a, n):
    return lax.div(a, jnp.int32(n))


def kernel(
    cls, tri, sub, pc, wp, prior, curves, weight, phase, out,
    bank, wloc, wrecv, wbuf, cosr, sinr, sbuf, acc0, acc1, ebuf, rbuf,
    lsem, ysend, yrecv, zsend, zrecv, xsend, xrecv, psend, precv, hsend, hrecv, csend, crecv, esend, erecv,
):
    grp = lax.axis_index("grp")
    blk = lax.axis_index("blk")
    x, zl, core = div(grp, 4), rem(div(grp, 2), 2), rem(grp, 2)
    zh, y = div(blk, 8), rem(blk, 8)
    z = zh * 2 + zl

    def dev(x_=x, z_=z, core_=core, y_=y):
        return ((x_ * 2 + rem(z_, 2)) * 2 + core_, div(z_, 2) * 8 + y_)

    partner = dev(core_=1 - core)
    yr, yl = dev(y_=rem(y + 1, NY)), dev(y_=rem(y + NY - 1, NY))
    zr, zlft = dev(z_=rem(z + 1, NZ)), dev(z_=rem(z + NZ - 1, NZ))
    xp = [dev(x_=rem(x + d, NX)) for d in (1, 2, 3)]
    ep = [dev(z_=rem(z + 2 * d, NZ)) for d in (1, 2, 3)]

    barrier = pltpu.get_barrier_semaphore()
    peers = [partner, yr, yl, zr, zlft] + xp
    for p in peers:
        pl.semaphore_signal(barrier, inc=1, device_id=p, device_id_type=MESH)

    f32, bf16 = jnp.float32, jnp.bfloat16
    k = curves.shape[1]
    first_rows = lax.broadcasted_iota(jnp.int32, (4, 1), 0) < 2
    nothing = jnp.zeros((1, (MAIN + 1) * LANES - k), f32)

    def curve_row(p):
        total = jnp.zeros((8, k), f32)
        for g in range(curves.shape[0] // 8):
            chosen = lax.broadcasted_iota(jnp.int32, (8, 1), 0) + 8 * g == cls[p]
            total = jnp.where(chosen, curves[pl.ds(8 * g, 8), :], total)
        row = jnp.sum(total, axis=0, keepdims=True)
        return jnp.concatenate([row * weight[...], nothing], axis=1)

    scaled = wp[...].astype(f32) * jnp.where(first_rows, curve_row(0), curve_row(1))
    lane4 = lax.broadcasted_iota(jnp.int32, (4, LANES), 1)
    part4 = lax.broadcasted_iota(jnp.int32, (4, LANES), 0) % 2
    own_class = jnp.where(first_rows, cls[0], cls[1])
    hit = (lane4 == own_class) | ((lane4 == own_class + 64) & (part4 == 0))
    wide = jnp.concatenate(
        [
            scaled[:, : MAIN * LANES],
            scaled[:, MAIN * LANES :] + prior[...].astype(f32),
            jnp.where(hit, 1.0, 0.0),
        ],
        axis=1,
    ).astype(bf16)
    wloc[0] = wide[:, :KH]
    wloc[1] = wide[:, KE - KH :]
    pl.semaphore_wait(barrier, len(peers))

    started = []

    def send(src, dst, ss, rs, to):
        c = pltpu.make_async_remote_copy(
            src_ref=src, dst_ref=dst, send_sem=ss, recv_sem=rs, device_id=to, device_id_type=MESH
        )
        c.start()
        started.append(c)

    def arrive(dst, ss, rs, frm):
        pltpu.make_async_remote_copy(
            src_ref=dst, dst_ref=dst, send_sem=ss, recv_sem=rs, device_id=frm, device_id_type=MESH
        ).wait_recv()

    def lanes(q):
        return pl.ds(PIECES[q][0] * LANES, PIECES[q][1] * LANES)

    def in_step(s, d, q):
        return s < 4 or (q < NQ // 2) == (d == 0)

    def y_send(s, q):
        for d, to in ((0, yr), (1, yl)):
            if in_step(s, d, q):
                y_send1(s, q, d, to)

    def slot(s, d):
        return (NY - s) % NY if d == 0 else s

    def y_send1(s, q, d, to):
        src = (bank.at[slot(s - 1, d)] if s > 1 or q == NQ - 1 else pc).at[:, lanes(q)]
        send(src, bank.at[slot(s, d), :, lanes(q)], ysend.at[d, s - 1, q], yrecv.at[d, s - 1, q], to)

    def y_step(s, pieces=range(NQ)):
        for q in pieces:
            for d, to in ((0, yr), (1, yl)):
                if in_step(s, d, q):
                    arrive(
                        bank.at[slot(s, d), :, lanes(q)],
                        ysend.at[d, s - 1, q], yrecv.at[d, s - 1, q], to,
                    )
                    if s < 4 and in_step(s + 1, d, q):
                        y_send1(s + 1, q, d, to)

    def at_x(g):
        return rem(x + g + NX, NX)

    def unit_a(half, o, g):
        return wbuf.at[half, div(o, 2), at_x(-g), rem(o, 2)]

    def plane_a(half, o):
        return wbuf.at[half, div(o, 2), :, rem(o, 2)]

    def z_origin(s, d):
        return rem(z + (NZ - s if d == 0 else s), NZ)

    def z_send(s, d, g):
        if s < 4 or (g < 2) == (d == 0):
            ref = unit_a(core, z_origin(s - 1, d), g)
            send(ref, ref, zsend.at[d, s - 1, g], zrecv.at[d, s - 1, g], zr if d == 0 else zlft)

    def z_step(s):
        for g in range(NX):
            for d in (0, 1):
                if s < 4 or (g < 2) == (d == 0):
                    ref = unit_a(core, z_origin(s, d), g)
                    arrive(ref, zsend.at[d, s - 1, g], zrecv.at[d, s - 1, g], zr)
                    if s < 4:
                        z_send(s + 1, d, g)
                    else:
                        send(ref, ref, hsend.at[g], hrecv.at[g], partner)
        if s < 4:
            for d in (0, 1):
                p_send(s, d)

    def p_send(s, d):
        ref = plane_a(core, z_origin(s, d))
        send(ref, ref, psend.at[d, s], precv.at[d, s], partner)

    def p_wait(s, d):
        arrive(plane_a(1 - core, z_origin(s, d)), psend.at[d, s], precv.at[d, s], partner)

    def shift(slot0):
        def body(i, carry):
            at = pl.ds(pl.multiple_of(i * LANES, LANES), LANES)
            both = [bank[slot0 + c, :, at].astype(f32) for c in (0, 1)]
            for t in range(NT):
                cos = jnp.broadcast_to(cosr[pl.ds(t, 1), at], (PJ, LANES))
                sin = jnp.broadcast_to(sinr[pl.ds(t, 1), at], (PJ, LANES))
                rows = pl.ds(t * NJ + slot0 * PJ, 2 * PJ)
                real = [cos * b[:PJ] + sin * b[PJ:] for b in both]
                imag = [cos * b[PJ:] - sin * b[:PJ] for b in both]
                sbuf[0, rows, at] = jnp.concatenate(real, axis=0).astype(bf16)
                sbuf[1, rows, at] = jnp.concatenate(imag, axis=0).astype(bf16)
            return carry

        lax.fori_loop(0, KE // LANES, body, 0)

    send(wloc.at[1 - core], wrecv, csend, crecv, partner)
    for q in range(NQ - 1):
        y_send(1, q)
    local = pltpu.make_async_copy(
        pc.at[:, pl.ds(0, MAIN * LANES)], bank.at[0, :, pl.ds(0, MAIN * LANES)], lsem
    )
    local.start()
    arrive(wrecv, csend, crecv, partner)
    mine = wloc[core].astype(jnp.float32)
    theirs = wrecv[...].astype(jnp.float32)
    first = jnp.where(core == 0, mine, theirs)
    second = jnp.where(core == 0, theirs, mine)
    wbuf[core, zh, x, zl] = jnp.concatenate([first, second], axis=0).astype(jnp.bfloat16)
    own = unit_a(core, z, 0)
    for d in range(3):
        send(own, own, xsend.at[d], xrecv.at[d], xp[d])
    for d in (0, 1):
        z_send(1, d, 0)
    both = pc[...].astype(f32)
    power = both[:PJ] * both[:PJ] + both[PJ:] * both[PJ:]
    curve_sq = curves[...] * weight[...] * curves[...]
    norm = -0.5 * lax.dot_general(
        power[:, :k], curve_sq, (((1,), (1,)), ((), ())),
        precision=lax.Precision.HIGHEST, preferred_element_type=f32,
    )
    high = norm.astype(bf16).astype(f32)
    mid = (norm - high).astype(bf16).astype(f32)
    low = norm - high - mid
    lane16 = lax.broadcasted_iota(jnp.int32, (2 * PJ, LANES), 1)
    row16 = lax.broadcasted_iota(jnp.int32, (2 * PJ, 1), 0)
    target = jnp.zeros((2 * PJ, 1), jnp.int32)
    for j in range(PJ):
        target = jnp.where(row16 == j, sub[j] + 32, target)
        target = jnp.where(row16 == PJ + j, sub[j] - 64, target)
    subset = jnp.where((lane16 == target) & (lane16 >= 32), 1.0, 0.0)
    bank[0, :, pl.ds(MAIN * LANES, LANES)] = (both[:, MAIN * LANES :] + subset).astype(bf16)
    terms = jnp.concatenate(
        [
            jnp.concatenate([high, mid], axis=1),
            jnp.concatenate([low, jnp.zeros_like(low)], axis=1),
        ],
        axis=0,
    )
    bank[0, :, pl.ds((MAIN + 1) * LANES, LANES)] = terms.astype(bf16)
    y_send(1, NQ - 1)
    y_step(1, range(NQ - 1))
    table = jnp.concatenate([phase[...], jnp.zeros((NT, KE - k), f32)], axis=1)
    row9 = lax.broadcasted_iota(jnp.int32, (NT, 1), 0)
    wanted = jnp.zeros((NT, 1), jnp.int32)
    for t in range(NT):
        wanted = jnp.where(row9 == t, tri[t], wanted)
    angle = jnp.zeros((NT, KE), f32)
    for t in range(NT):
        angle = jnp.where(wanted == t, table[t : t + 1], angle)
    cosr[...] = jnp.cos(angle)
    sinr[...] = jnp.sin(angle)
    y_step(1, (NQ - 1,))
    for g in range(1, NX):
        arrive(unit_a(core, z, g), xsend.at[g - 1], xrecv.at[g - 1], xp[g - 1])
        z_send(1, 0, g)
        z_send(1, 1, g)
    p_send(0, 0)
    z_step(1)
    local.wait()
    shift(0)
    y_step(2)
    z_step(2)
    shift(6)
    y_step(3)
    z_step(3)
    shift(2)
    y_step(4)
    shift(4)
    p_wait(0, 0)
    for s in range(1, 4):
        for d in (0, 1):
            p_wait(s, d)

    dims = (((1,), (1,)), ((), ()))

    def cross(part, acc, blocks):
        fresh = True
        for kh, first, tiles, base in ((0, 0, 8, 0), (0, 8, 8, 0), (1, 0, 8, 16), (1, 8, 9, 16)):
            at = pl.ds(first * LANES, tiles * LANES)
            w = [
                wbuf[kh, rem(zh + d, NZH), :, :, :, at].reshape(ROWS // NZH, tiles * LANES)
                for d in blocks
            ]
            w = jnp.concatenate(w, axis=0) if len(w) > 1 else w[0]
            sh = sbuf[part, :, pl.ds((base + first) * LANES, tiles * LANES)]
            prod = lax.dot_general(w, sh, dims, preferred_element_type=f32)
            fill = jnp.zeros((prod.shape[0], NS * LANES - NT * NJ), f32)
            prod = jnp.concatenate([prod, fill], axis=1)
            for m in range(NS):
                for n, d in enumerate(blocks):
                    slab = prod[n * 64 : (n + 1) * 64, m * LANES : (m + 1) * LANES]
                    rows = pl.ds(d * 64, 64)
                    acc[m, rows, :] = slab if fresh else acc[m, rows, :] + slab
            fresh = False

    def finish(blocks):
        cross(0, acc0, blocks)
        cross(1, acc1, blocks)
        for d in blocks:
            for m in range(NS):
                val = (
                    acc0[m, pl.ds(d * 64, 32, stride=2), :]
                    + acc1[m, pl.ds(d * 64 + 1, 32, stride=2), :]
                )
                if d == 0:
                    rbuf[zh, m] = val
                else:
                    ebuf[d - 1, m] = val
            if d:
                send(ebuf.at[d - 1], rbuf.at[zh], esend.at[d - 1], erecv.at[d - 1], ep[d - 1])

    finish((1, 3, 0))
    z_step(4)
    for g in range(NX):
        arrive(unit_a(1 - core, z_origin(4, 0), g), hsend.at[g], hrecv.at[g], partner)
    finish((2,))

    left = lax.broadcasted_iota(jnp.int32, (32, LANES), 1) < NJ

    def turned(m):
        for slab in range(NS):
            val = rbuf[m, slab]
            swapped = pltpu.roll(val, NJ, 1)
            yield pltpu.roll(jnp.where(left, val, swapped), PJ * y, 1)
            yield pltpu.roll(jnp.where(left, swapped, val), PJ * y, 1)

    for d in (1, 3, 2):
        arrive(rbuf.at[rem(zh + NZH - d, NZH)], esend.at[d - 1], erecv.at[d - 1], ep[d - 1])
    for m in range(0, NZH, 2):
        for t, low, high in zip(range(NT), turned(m), turned(m + 1)):
            out[t, :, pl.ds(m * NJ, LANES)] = jnp.where(left, low, high)
    for c in started:
        c.wait_send()


def per_device(
    particles,
    ctf_class,
    orient_prior,
    ctf_curves,
    noise_weight,
    shift_phase,
    trans_index,
    projections,
    orient_subset,
):
    f32, bf16 = jnp.float32, jnp.bfloat16
    k = ctf_curves.shape[1]
    fill = (MAIN + 1) * LANES - k
    pc = jnp.concatenate([projections[:, 0, :], projections[:, 1, :]], axis=0)
    pc = jnp.pad(pc, ((0, 0), (0, fill)))
    wp = jnp.pad(particles.reshape(4, k), ((0, 0), (0, fill)))
    prior = jnp.pad(orient_prior.reshape(4, fill), ((0, 0), (LANES - fill, 0)))

    dma = pltpu.SemaphoreType.DMA
    vm = pl.BlockSpec(memory_space=pltpu.VMEM)
    sm = pl.BlockSpec(memory_space=pltpu.SMEM)
    scores = pl.pallas_call(
        kernel,
        out_shape=jax.ShapeDtypeStruct((NT, 32, NZH * NJ), f32),
        in_specs=[sm] * 3 + [vm] * 6,
        out_specs=vm,
        scratch_shapes=[
            pltpu.VMEM((NY, 2 * PJ, KE), bf16),
            pltpu.VMEM((2, 4, KH), bf16),
            pltpu.VMEM((4, KH), bf16),
            pltpu.VMEM((2, NZH, NX, NZL, 8, KH), bf16),
            pltpu.VMEM((NT, KE), f32),
            pltpu.VMEM((NT, KE), f32),
            pltpu.VMEM((2, NT * NJ, KE), bf16),
            pltpu.VMEM((NS, ROWS, LANES), f32),
            pltpu.VMEM((NS, ROWS, LANES), f32),
            pltpu.VMEM((3, NS, 32, LANES), f32),
            pltpu.VMEM((NZH, NS, 32, LANES), f32),
            dma,
            dma((2, 4, NQ)),
            dma((2, 4, NQ)),
            dma((2, 4, NX)),
            dma((2, 4, NX)),
            dma((3,)),
            dma((3,)),
            dma((2, 4)),
            dma((2, 4)),
            dma((NX,)),
            dma((NX,)),
            dma,
            dma,
            dma((3,)),
            dma((3,)),
        ],
        compiler_params=pltpu.CompilerParams(
            collective_id=0, has_side_effects=True, vmem_limit_bytes=48 << 20
        ),
        name="scores",
    )(
        ctf_class, trans_index, orient_subset,
        pc, wp, prior, ctf_curves, noise_weight[None, :], shift_phase,
    )
    return jnp.transpose(scores, (1, 0, 2))


def solution(mesh):
    placed = (
        P(("blk", "grp"), None, None),
        P(("blk", "grp")),
        P(("blk", "grp"), None),
        P(),
        P(),
        P(),
        P(),
        P(("grp", "blk"), None, None),
        P(("grp", "blk")),
    )
    return jax.shard_map(
        per_device, mesh=mesh, in_specs=placed, out_specs=P("blk", None, "grp"), check_vma=False
    )
```

```python
import jax
import jax.numpy as jnp
from jax import lax
from jax.experimental import pallas as pl
from jax.experimental.pallas import tpu as pltpu
from jax.sharding import PartitionSpec as P

MESH = pl.DeviceIdType.MESH
NX, NZL, NC, NZH, NY = 4, 2, 2, 4, 8
NZ = NZH * NZL
NT = 9
PJ = 8
LANES = 128
KE = 33 * LANES
KH = 17 * LANES
MAIN = 31
PIECES = ((0, 10), (10, 10), (20, 11), (31, 2))
NQ = len(PIECES)
NJ = NY * PJ
NS = 5
NJ = NY * PJ
EARLY, LATE = (7, 0, 1), (2, 3, 4, 5, 6)
GROUPS = ((EARLY, 0, 2), (LATE, 2, 3))
SPANS = ((0, 0, 8, 0), (0, 8, 8, 0), (1, 0, 8, 16), (1, 8, 9, 16))
CHUNKS = ((0, 256), (2, 256), (4, 64))
ROWS = NZ * NX * 8


def rem(a, n):
    return lax.rem(a, jnp.int32(n))


def div(a, n):
    return lax.div(a, jnp.int32(n))


def kernel(
    cls, tri, sub, pc, wp, prior, curves, weight, phase, out,
    bank, wloc, wrecv, wbuf, cosr, sinr, sbuf, acc0, acc1, ebuf, rbuf,
    lsem, ysend, yrecv, zsend, zrecv, xsend, xrecv, psend, precv, hsend, hrecv, csend, crecv, esend, erecv,
):
    grp = lax.axis_index("grp")
    blk = lax.axis_index("blk")
    x, zl, core = div(grp, 4), rem(div(grp, 2), 2), rem(grp, 2)
    zh, y = div(blk, 8), rem(blk, 8)
    z = zh * 2 + zl

    def dev(x_=x, z_=z, core_=core, y_=y):
        return ((x_ * 2 + rem(z_, 2)) * 2 + core_, div(z_, 2) * 8 + y_)

    partner = dev(core_=1 - core)
    yr, yl = dev(y_=rem(y + 1, NY)), dev(y_=rem(y + NY - 1, NY))
    zr, zlft = dev(z_=rem(z + 1, NZ)), dev(z_=rem(z + NZ - 1, NZ))
    xp = [dev(x_=rem(x + d, NX)) for d in (1, 2, 3)]
    ep = [dev(z_=rem(z + 2 * d, NZ)) for d in (1, 2, 3)]

    barrier = pltpu.get_barrier_semaphore()
    peers = [partner, yr, yl, zr, zlft] + xp
    for p in peers:
        pl.semaphore_signal(barrier, inc=1, device_id=p, device_id_type=MESH)

    f32, bf16 = jnp.float32, jnp.bfloat16
    k = curves.shape[1]
    first_rows = lax.broadcasted_iota(jnp.int32, (4, 1), 0) < 2

    def curve_row(p):
        total = jnp.zeros((8, k), f32)
        for g in range(curves.shape[0] // 8):
            chosen = lax.broadcasted_iota(jnp.int32, (8, 1), 0) + 8 * g == cls[p]
            total = jnp.where(chosen, curves[pl.ds(8 * g, 8), :], total)
        row = jnp.sum(total, axis=0, keepdims=True)
        return row * weight[...]

    rows4 = jnp.concatenate([wp[0].astype(f32), wp[1].astype(f32)], axis=0)
    scaled = rows4 * jnp.where(first_rows, curve_row(0), curve_row(1))
    prior_f = prior[...].astype(f32)
    half = prior.shape[1] // 2
    prior4 = jnp.concatenate(
        [prior_f[p : p + 1, h * half : (h + 1) * half] for p in (0, 1) for h in (0, 1)], axis=0
    )
    lane4 = lax.broadcasted_iota(jnp.int32, (4, LANES), 1)
    part4 = lax.broadcasted_iota(jnp.int32, (4, LANES), 0) % 2
    own_class = jnp.where(first_rows, cls[0], cls[1])
    hit = (lane4 == own_class) | ((lane4 == own_class + 64) & (part4 == 0))
    wide = jnp.concatenate([scaled, prior4, jnp.where(hit, 1.0, 0.0)], axis=1).astype(bf16)
    wloc[0] = wide[:, :KH]
    wloc[1] = wide[:, KE - KH :]
    pl.semaphore_wait(barrier, len(peers))

    started = []

    def send(src, dst, ss, rs, to):
        c = pltpu.make_async_remote_copy(
            src_ref=src, dst_ref=dst, send_sem=ss, recv_sem=rs, device_id=to, device_id_type=MESH
        )
        c.start()
        started.append(c)

    def arrive(dst, ss, rs, frm):
        pltpu.make_async_remote_copy(
            src_ref=dst, dst_ref=dst, send_sem=ss, recv_sem=rs, device_id=frm, device_id_type=MESH
        ).wait_recv()

    def lanes(q):
        return pl.ds(PIECES[q][0] * LANES, PIECES[q][1] * LANES)

    def in_step(s, d, q):
        return s < 4 or (q < NQ // 2) == (d == 0)

    def y_send(s, q):
        for d, to in ((0, yr), (1, yl)):
            if in_step(s, d, q):
                y_send1(s, q, d, to)

    def slot(s, d):
        return (NY - s) % NY if d == 0 else s

    def y_send1(s, q, d, to):
        src = (bank.at[slot(s - 1, d)] if s > 1 or q == NQ - 1 else pc).at[:, lanes(q)]
        send(src, bank.at[slot(s, d), :, lanes(q)], ysend.at[d, s - 1, q], yrecv.at[d, s - 1, q], to)

    def y_step(s, pieces=range(NQ)):
        for q in pieces:
            for d, to in ((0, yr), (1, yl)):
                if in_step(s, d, q):
                    arrive(
                        bank.at[slot(s, d), :, lanes(q)],
                        ysend.at[d, s - 1, q], yrecv.at[d, s - 1, q], to,
                    )
                    if s < 4 and in_step(s + 1, d, q):
                        y_send1(s + 1, q, d, to)

    def at_x(g):
        return rem(x + g + NX, NX)

    def unit_a(half, o, g):
        return wbuf.at[half, div(o, 2), at_x(-g), rem(o, 2)]

    def plane_a(half, o):
        return wbuf.at[half, div(o, 2), :, rem(o, 2)]

    def z_origin(s, d):
        return rem(z + (NZ - s if d == 0 else s), NZ)

    def z_send(s, d, g):
        if s < 4 or (g < 2) == (d == 0):
            ref = unit_a(core, z_origin(s - 1, d), g)
            send(ref, ref, zsend.at[d, s - 1, g], zrecv.at[d, s - 1, g], zr if d == 0 else zlft)

    def z_step(s):
        for g in range(NX):
            for d in (0, 1):
                if s < 4 or (g < 2) == (d == 0):
                    ref = unit_a(core, z_origin(s, d), g)
                    arrive(ref, zsend.at[d, s - 1, g], zrecv.at[d, s - 1, g], zr)
                    if s < 4:
                        z_send(s + 1, d, g)
                    else:
                        send(ref, ref, hsend.at[g], hrecv.at[g], partner)
        if s < 4:
            for d in (0, 1):
                p_send(s, d)

    def p_send(s, d):
        ref = plane_a(core, z_origin(s, d))
        send(ref, ref, psend.at[d, s], precv.at[d, s], partner)

    def p_wait(s, d):
        arrive(plane_a(1 - core, z_origin(s, d)), psend.at[d, s], precv.at[d, s], partner)

    def shift(slot0):
        def body(i, carry):
            at = pl.ds(pl.multiple_of(i * LANES, LANES), LANES)
            both = [bank[slot0 + c, :, at].astype(f32) for c in (0, 1)]
            for t in range(NT):
                cos = jnp.broadcast_to(cosr[pl.ds(t, 1), at], (PJ, LANES))
                sin = jnp.broadcast_to(sinr[pl.ds(t, 1), at], (PJ, LANES))
                rows = pl.ds(t * NJ + slot0 * PJ, 2 * PJ)
                real = [cos * b[:PJ] + sin * b[PJ:] for b in both]
                imag = [cos * b[PJ:] - sin * b[:PJ] for b in both]
                sbuf[0, rows, at] = jnp.concatenate(real, axis=0).astype(bf16)
                sbuf[1, rows, at] = jnp.concatenate(imag, axis=0).astype(bf16)
            return carry

        lax.fori_loop(0, KE // LANES, body, 0)

    send(wloc.at[1 - core], wrecv, csend, crecv, partner)
    for q in range(NQ - 1):
        y_send(1, q)
    local = pltpu.make_async_copy(
        pc.at[:, pl.ds(0, MAIN * LANES)], bank.at[0, :, pl.ds(0, MAIN * LANES)], lsem
    )
    local.start()
    arrive(wrecv, csend, crecv, partner)
    mine = wloc[core].astype(jnp.float32)
    theirs = wrecv[...].astype(jnp.float32)
    first = jnp.where(core == 0, mine, theirs)
    second = jnp.where(core == 0, theirs, mine)
    wbuf[core, zh, x, zl] = jnp.concatenate([first, second], axis=0).astype(jnp.bfloat16)
    own = unit_a(core, z, 0)
    for d in range(3):
        send(own, own, xsend.at[d], xrecv.at[d], xp[d])
    for d in (0, 1):
        z_send(1, d, 0)
    both = pc[...].astype(f32)
    power = both[:PJ] * both[:PJ] + both[PJ:] * both[PJ:]
    curve_sq = curves[...] * weight[...] * curves[...]
    norm = -0.5 * lax.dot_general(
        power[:, :k], curve_sq, (((1,), (1,)), ((), ())),
        precision=lax.Precision.HIGHEST, preferred_element_type=f32,
    )
    high = norm.astype(bf16).astype(f32)
    mid = (norm - high).astype(bf16).astype(f32)
    low = norm - high - mid
    lane16 = lax.broadcasted_iota(jnp.int32, (2 * PJ, LANES), 1)
    row16 = lax.broadcasted_iota(jnp.int32, (2 * PJ, 1), 0)
    target = jnp.zeros((2 * PJ, 1), jnp.int32)
    for j in range(PJ):
        target = jnp.where(row16 == j, sub[j] + 32, target)
        target = jnp.where(row16 == PJ + j, sub[j] - 64, target)
    subset = jnp.where((lane16 == target) & (lane16 >= 32), 1.0, 0.0)
    bank[0, :, pl.ds(MAIN * LANES, LANES)] = (both[:, MAIN * LANES :] + subset).astype(bf16)
    terms = jnp.concatenate(
        [
            jnp.concatenate([high, mid], axis=1),
            jnp.concatenate([low, jnp.zeros_like(low)], axis=1),
        ],
        axis=0,
    )
    bank[0, :, pl.ds((MAIN + 1) * LANES, LANES)] = terms.astype(bf16)
    y_send(1, NQ - 1)
    y_step(1, range(NQ - 1))
    table = jnp.concatenate([phase[...], jnp.zeros((NT, KE - k), f32)], axis=1)
    row9 = lax.broadcasted_iota(jnp.int32, (NT, 1), 0)
    wanted = jnp.zeros((NT, 1), jnp.int32)
    for t in range(NT):
        wanted = jnp.where(row9 == t, tri[t], wanted)
    angle = jnp.zeros((NT, KE), f32)
    for t in range(NT):
        angle = jnp.where(wanted == t, table[t : t + 1], angle)
    cosr[...] = jnp.cos(angle)
    sinr[...] = jnp.sin(angle)
    y_step(1, (NQ - 1,))
    for g in range(1, NX):
        arrive(unit_a(core, z, g), xsend.at[g - 1], xrecv.at[g - 1], xp[g - 1])
        z_send(1, 0, g)
        z_send(1, 1, g)
    p_send(0, 0)
    z_step(1)
    local.wait()
    shift(0)
    y_step(2)
    z_step(2)
    shift(6)
    y_step(3)
    z_step(3)
    shift(2)
    y_step(4)
    shift(4)
    p_wait(0, 0)
    for s in range(1, 4):
        for d in (0, 1):
            p_wait(s, d)

    dims = (((1,), (1,)), ((), ()))

    def cross(part, acc, blocks, lo, count):
        fresh = True
        for kh, first, tiles, base in SPANS:
            at = pl.ds(first * LANES, tiles * LANES)
            w = [
                wbuf[kh, rem(zh + d, NZH), :, :, :, at].reshape(ROWS // NZH, tiles * LANES)
                for d in blocks
            ]
            w = jnp.concatenate(w, axis=0) if len(w) > 1 else w[0]
            sh = sbuf[part, pl.ds(lo * LANES, count), pl.ds((base + first) * LANES, tiles * LANES)]
            prod = lax.dot_general(w, sh, dims, preferred_element_type=f32)
            if count % LANES:
                fill = jnp.zeros((prod.shape[0], LANES - count % LANES), f32)
                prod = jnp.concatenate([prod, fill], axis=1)
            for m in range(prod.shape[1] // LANES):
                for n, d in enumerate(blocks):
                    slab = prod[n * 64 : (n + 1) * 64, m * LANES : (m + 1) * LANES]
                    rows = pl.ds(d * 64, 64)
                    acc[lo + m, rows, :] = slab if fresh else acc[lo + m, rows, :] + slab
            fresh = False

    def finish(blocks):
        for i, (lo, count) in enumerate(CHUNKS):
            cross(0, acc0, blocks, lo, count)
            cross(1, acc1, blocks, lo, count)
            slabs = (count + LANES - 1) // LANES
            for d in blocks:
                for m in range(lo, lo + slabs):
                    val = (
                        acc0[m, pl.ds(d * 64, 32, stride=2), :]
                        + acc1[m, pl.ds(d * 64 + 1, 32, stride=2), :]
                    )
                    if d == 0:
                        rbuf[zh, m] = val
                    else:
                        ebuf[d - 1, m] = val
                if d:
                    at = pl.ds(lo, slabs)
                    send(
                        ebuf.at[d - 1, at], rbuf.at[zh, at],
                        esend.at[d - 1, i], erecv.at[d - 1, i], ep[d - 1],
                    )

    z_step(4)
    finish((1, 3, 0))
    for g in range(NX):
        arrive(unit_a(1 - core, z_origin(4, 0), g), hsend.at[g], hrecv.at[g], partner)
    finish((2,))

    left = lax.broadcasted_iota(jnp.int32, (32, LANES), 1) < NJ

    def turned(m):
        for slab in range(NS):
            val = rbuf[m, slab]
            swapped = pltpu.roll(val, NJ, 1)
            yield pltpu.roll(jnp.where(left, val, swapped), PJ * y, 1)
            yield pltpu.roll(jnp.where(left, swapped, val), PJ * y, 1)

    for d in (1, 3, 2):
        for i, (lo, count) in enumerate(CHUNKS):
            block = rbuf.at[rem(zh + NZH - d, NZH), pl.ds(lo, (count + LANES - 1) // LANES)]
            arrive(block, esend.at[d - 1, i], erecv.at[d - 1, i], ep[d - 1])
    for m in range(0, NZH, 2):
        for t, low, high in zip(range(NT), turned(m), turned(m + 1)):
            out[t, :, pl.ds(m * NJ, LANES)] = jnp.where(left, low, high)
    for c in started:
        c.wait_send()


def per_device(
    particles,
    ctf_class,
    orient_prior,
    ctf_curves,
    noise_weight,
    shift_phase,
    trans_index,
    projections,
    orient_subset,
):
    f32, bf16 = jnp.float32, jnp.bfloat16
    k = ctf_curves.shape[1]
    fill = (MAIN + 1) * LANES - k
    pc = jnp.concatenate([projections[:, 0, :], projections[:, 1, :]], axis=0)
    pc = jnp.pad(pc, ((0, 0), (0, fill)))

    dma = pltpu.SemaphoreType.DMA
    vm = pl.BlockSpec(memory_space=pltpu.VMEM)
    sm = pl.BlockSpec(memory_space=pltpu.SMEM)
    scores = pl.pallas_call(
        kernel,
        out_shape=jax.ShapeDtypeStruct((NT, 32, NZH * NJ), f32),
        in_specs=[sm] * 3 + [vm] * 6,
        out_specs=vm,
        scratch_shapes=[
            pltpu.VMEM((NY, 2 * PJ, KE), bf16),
            pltpu.VMEM((2, 4, KH), bf16),
            pltpu.VMEM((4, KH), bf16),
            pltpu.VMEM((2, NZH, NX, NZL, 8, KH), bf16),
            pltpu.VMEM((NT, KE), f32),
            pltpu.VMEM((NT, KE), f32),
            pltpu.VMEM((2, NT * NJ, KE), bf16),
            pltpu.VMEM((NS, ROWS, LANES), f32),
            pltpu.VMEM((NS, ROWS, LANES), f32),
            pltpu.VMEM((3, NS, 32, LANES), f32),
            pltpu.VMEM((NZH, NS, 32, LANES), f32),
            dma,
            dma((2, 4, NQ)),
            dma((2, 4, NQ)),
            dma((2, 4, NX)),
            dma((2, 4, NX)),
            dma((3,)),
            dma((3,)),
            dma((2, 4)),
            dma((2, 4)),
            dma((NX,)),
            dma((NX,)),
            dma,
            dma,
            dma((3, len(CHUNKS))),
            dma((3, len(CHUNKS))),
        ],
        compiler_params=pltpu.CompilerParams(
            collective_id=0, has_side_effects=True, vmem_limit_bytes=48 << 20
        ),
        name="scores",
    )(
        ctf_class, trans_index, orient_subset,
        pc, particles, orient_prior, ctf_curves, noise_weight[None, :], shift_phase,
    )
    return jnp.transpose(scores, (1, 0, 2))


def solution(mesh):
    placed = (
        P(("blk", "grp"), None, None),
        P(("blk", "grp")),
        P(("blk", "grp"), None),
        P(),
        P(),
        P(),
        P(),
        P(("grp", "blk"), None, None),
        P(("grp", "blk")),
    )
    return jax.shard_map(
        per_device, mesh=mesh, in_specs=placed, out_specs=P("blk", None, "grp"), check_vma=False
    )
```

```python
import jax
import jax.numpy as jnp
from jax import lax
from jax.experimental import pallas as pl
from jax.experimental.pallas import tpu as pltpu
from jax.sharding import PartitionSpec as P

MESH = pl.DeviceIdType.MESH
NX, NZL, NC, NZH, NY = 4, 2, 2, 4, 8
NZ = NZH * NZL
NT = 9
PJ = 8
LANES = 128
KE = 33 * LANES
KH = 17 * LANES
MAIN = 31
PIECES = ((0, 10), (10, 10), (20, 11), (31, 2))
NQ = len(PIECES)
NJ = NY * PJ
NS = 5
NJ = NY * PJ
EARLY, LATE = (7, 0, 1), (2, 3, 4, 5, 6)
GROUPS = ((EARLY, 0, 2), (LATE, 2, 3))
SPANS = ((0, 0, 8, 0), (0, 8, 8, 0), (1, 0, 8, 16), (1, 8, 9, 16))
CHUNKS = ((0, 256), (2, 256), (4, 64))
ROWS = NZ * NX * 8


def rem(a, n):
    return lax.rem(a, jnp.int32(n))


def div(a, n):
    return lax.div(a, jnp.int32(n))


def kernel(
    cls, tri, sub, pc, wp, prior, curves, weight, phase, out,
    bank, wloc, wrecv, wbuf, cosr, sinr, sbuf, acc0, acc1, ebuf, rbuf,
    lsem, ysend, yrecv, zsend, zrecv, xsend, xrecv, psend, precv, hsend, hrecv, csend, crecv, esend, erecv,
):
    grp = lax.axis_index("grp")
    blk = lax.axis_index("blk")
    x, zl, core = div(grp, 4), rem(div(grp, 2), 2), rem(grp, 2)
    zh, y = div(blk, 8), rem(blk, 8)
    z = zh * 2 + zl

    def dev(x_=x, z_=z, core_=core, y_=y):
        return ((x_ * 2 + rem(z_, 2)) * 2 + core_, div(z_, 2) * 8 + y_)

    partner = dev(core_=1 - core)
    yr, yl = dev(y_=rem(y + 1, NY)), dev(y_=rem(y + NY - 1, NY))
    zr, zlft = dev(z_=rem(z + 1, NZ)), dev(z_=rem(z + NZ - 1, NZ))
    xp = [dev(x_=rem(x + d, NX)) for d in (1, 2, 3)]
    ep = [dev(z_=rem(z + 2 * d, NZ)) for d in (1, 2, 3)]

    barrier = pltpu.get_barrier_semaphore()
    peers = [partner, yr, yl, zr, zlft] + xp
    for p in peers:
        pl.semaphore_signal(barrier, inc=1, device_id=p, device_id_type=MESH)

    f32, bf16 = jnp.float32, jnp.bfloat16
    k = curves.shape[1]
    first_rows = lax.broadcasted_iota(jnp.int32, (4, 1), 0) < 2

    def curve_row(p):
        total = jnp.zeros((8, k), f32)
        for g in range(curves.shape[0] // 8):
            chosen = lax.broadcasted_iota(jnp.int32, (8, 1), 0) + 8 * g == cls[p]
            total = jnp.where(chosen, curves[pl.ds(8 * g, 8), :], total)
        row = jnp.sum(total, axis=0, keepdims=True)
        return row * weight[...]

    rows4 = jnp.concatenate([wp[0].astype(f32), wp[1].astype(f32)], axis=0)
    scaled = rows4 * jnp.where(first_rows, curve_row(0), curve_row(1))
    prior_f = prior[...].astype(f32)
    half = prior.shape[1] // 2
    prior4 = jnp.concatenate(
        [prior_f[p : p + 1, h * half : (h + 1) * half] for p in (0, 1) for h in (0, 1)], axis=0
    )
    lane4 = lax.broadcasted_iota(jnp.int32, (4, LANES), 1)
    part4 = lax.broadcasted_iota(jnp.int32, (4, LANES), 0) % 2
    own_class = jnp.where(first_rows, cls[0], cls[1])
    hit = (lane4 == own_class) | ((lane4 == own_class + 64) & (part4 == 0))
    wide = jnp.concatenate([scaled, prior4, jnp.where(hit, 1.0, 0.0)], axis=1).astype(bf16)
    wloc[0] = wide[:, :KH]
    wloc[1] = wide[:, KE - KH :]
    pl.semaphore_wait(barrier, len(peers))

    started = []

    def send(src, dst, ss, rs, to):
        c = pltpu.make_async_remote_copy(
            src_ref=src, dst_ref=dst, send_sem=ss, recv_sem=rs, device_id=to, device_id_type=MESH
        )
        c.start()
        started.append(c)

    def arrive(dst, ss, rs, frm):
        pltpu.make_async_remote_copy(
            src_ref=dst, dst_ref=dst, send_sem=ss, recv_sem=rs, device_id=frm, device_id_type=MESH
        ).wait_recv()

    def lanes(q):
        return pl.ds(PIECES[q][0] * LANES, PIECES[q][1] * LANES)

    def in_step(s, d, q):
        return s < 4 or (q < NQ // 2) == (d == 0)

    def y_send(s, q):
        for d, to in ((0, yr), (1, yl)):
            if in_step(s, d, q):
                y_send1(s, q, d, to)

    def slot(s, d):
        return (NY - s) % NY if d == 0 else s

    def y_send1(s, q, d, to):
        src = (bank.at[slot(s - 1, d)] if s > 1 or q == NQ - 1 else pc).at[:, lanes(q)]
        send(src, bank.at[slot(s, d), :, lanes(q)], ysend.at[d, s - 1, q], yrecv.at[d, s - 1, q], to)

    def y_step(s, pieces=range(NQ)):
        for q in pieces:
            for d, to in ((0, yr), (1, yl)):
                if in_step(s, d, q):
                    arrive(
                        bank.at[slot(s, d), :, lanes(q)],
                        ysend.at[d, s - 1, q], yrecv.at[d, s - 1, q], to,
                    )
                    if s < 4 and in_step(s + 1, d, q):
                        y_send1(s + 1, q, d, to)

    def at_x(g):
        return rem(x + g + NX, NX)

    def unit_a(half, o, g):
        return wbuf.at[half, div(o, 2), at_x(-g), rem(o, 2)]

    def plane_a(half, o):
        return wbuf.at[half, div(o, 2), :, rem(o, 2)]

    def z_origin(s, d):
        return rem(z + (NZ - s if d == 0 else s), NZ)

    def z_send(s, d, g):
        if s < 4 or (g < 2) == (d == 0):
            ref = unit_a(core, z_origin(s - 1, d), g)
            send(ref, ref, zsend.at[d, s - 1, g], zrecv.at[d, s - 1, g], zr if d == 0 else zlft)

    def z_step(s):
        for g in range(NX):
            for d in (0, 1):
                if s < 4 or (g < 2) == (d == 0):
                    ref = unit_a(core, z_origin(s, d), g)
                    arrive(ref, zsend.at[d, s - 1, g], zrecv.at[d, s - 1, g], zr)
                    if s < 4:
                        z_send(s + 1, d, g)
                    else:
                        send(ref, ref, hsend.at[g], hrecv.at[g], partner)
        if s < 4:
            for d in (0, 1):
                p_send(s, d)

    def p_send(s, d):
        ref = plane_a(core, z_origin(s, d))
        send(ref, ref, psend.at[d, s], precv.at[d, s], partner)

    def p_wait(s, d):
        arrive(plane_a(1 - core, z_origin(s, d)), psend.at[d, s], precv.at[d, s], partner)

    def shift(slot0):
        def body(i, carry):
            at = pl.ds(pl.multiple_of(i * LANES, LANES), LANES)
            both = [bank[slot0 + c, :, at].astype(f32) for c in (0, 1)]
            for t in range(NT):
                cos = jnp.broadcast_to(cosr[pl.ds(t, 1), at], (PJ, LANES))
                sin = jnp.broadcast_to(sinr[pl.ds(t, 1), at], (PJ, LANES))
                rows = pl.ds(t * NJ + slot0 * PJ, 2 * PJ)
                real = [cos * b[:PJ] + sin * b[PJ:] for b in both]
                imag = [cos * b[PJ:] - sin * b[:PJ] for b in both]
                sbuf[0, rows, at] = jnp.concatenate(real, axis=0).astype(bf16)
                sbuf[1, rows, at] = jnp.concatenate(imag, axis=0).astype(bf16)
            return carry

        lax.fori_loop(0, KE // LANES, body, 0)

    send(wloc.at[1 - core], wrecv, csend, crecv, partner)
    for q in range(NQ - 1):
        y_send(1, q)
    local = pltpu.make_async_copy(
        pc.at[:, pl.ds(0, MAIN * LANES)], bank.at[0, :, pl.ds(0, MAIN * LANES)], lsem
    )
    local.start()
    arrive(wrecv, csend, crecv, partner)
    mine = wloc[core].astype(jnp.float32)
    theirs = wrecv[...].astype(jnp.float32)
    first = jnp.where(core == 0, mine, theirs)
    second = jnp.where(core == 0, theirs, mine)
    wbuf[core, zh, x, zl] = jnp.concatenate([first, second], axis=0).astype(jnp.bfloat16)
    own = unit_a(core, z, 0)
    for d in range(3):
        send(own, own, xsend.at[d], xrecv.at[d], xp[d])
    for d in (0, 1):
        z_send(1, d, 0)
    both = pc[...].astype(f32)
    power = both[:PJ] * both[:PJ] + both[PJ:] * both[PJ:]
    curve_sq = curves[...] * weight[...] * curves[...]
    norm = -0.5 * lax.dot_general(
        power[:, :k], curve_sq, (((1,), (1,)), ((), ())),
        precision=lax.Precision.HIGHEST, preferred_element_type=f32,
    )
    high = norm.astype(bf16).astype(f32)
    mid = (norm - high).astype(bf16).astype(f32)
    low = norm - high - mid
    lane16 = lax.broadcasted_iota(jnp.int32, (2 * PJ, LANES), 1)
    row16 = lax.broadcasted_iota(jnp.int32, (2 * PJ, 1), 0)
    target = jnp.zeros((2 * PJ, 1), jnp.int32)
    for j in range(PJ):
        target = jnp.where(row16 == j, sub[j] + 32, target)
        target = jnp.where(row16 == PJ + j, sub[j] - 64, target)
    subset = jnp.where((lane16 == target) & (lane16 >= 32), 1.0, 0.0)
    bank[0, :, pl.ds(MAIN * LANES, LANES)] = (both[:, MAIN * LANES :] + subset).astype(bf16)
    terms = jnp.concatenate(
        [
            jnp.concatenate([high, mid], axis=1),
            jnp.concatenate([low, jnp.zeros_like(low)], axis=1),
        ],
        axis=0,
    )
    bank[0, :, pl.ds((MAIN + 1) * LANES, LANES)] = terms.astype(bf16)
    y_send(1, NQ - 1)
    y_step(1, range(NQ - 1))
    table = jnp.concatenate([phase[...], jnp.zeros((NT, KE - k), f32)], axis=1)
    row9 = lax.broadcasted_iota(jnp.int32, (NT, 1), 0)
    wanted = jnp.zeros((NT, 1), jnp.int32)
    for t in range(NT):
        wanted = jnp.where(row9 == t, tri[t], wanted)
    angle = jnp.zeros((NT, KE), f32)
    for t in range(NT):
        angle = jnp.where(wanted == t, table[t : t + 1], angle)
    cosr[...] = jnp.cos(angle)
    sinr[...] = jnp.sin(angle)
    y_step(1, (NQ - 1,))
    for g in range(1, NX):
        arrive(unit_a(core, z, g), xsend.at[g - 1], xrecv.at[g - 1], xp[g - 1])
        z_send(1, 0, g)
        z_send(1, 1, g)
    p_send(0, 0)
    z_step(1)
    local.wait()
    shift(0)
    y_step(2)
    z_step(2)
    y_step(3)
    shift(6)
    z_step(3)
    y_step(4)
    shift(2)
    shift(4)
    p_wait(0, 0)
    for s in range(1, 4):
        for d in (0, 1):
            p_wait(s, d)

    dims = (((1,), (1,)), ((), ()))

    def cross(part, acc, blocks, lo, count):
        fresh = True
        for kh, first, tiles, base in SPANS:
            at = pl.ds(first * LANES, tiles * LANES)
            w = [
                wbuf[kh, rem(zh + d, NZH), :, :, :, at].reshape(ROWS // NZH, tiles * LANES)
                for d in blocks
            ]
            w = jnp.concatenate(w, axis=0) if len(w) > 1 else w[0]
            sh = sbuf[part, pl.ds(lo * LANES, count), pl.ds((base + first) * LANES, tiles * LANES)]
            prod = lax.dot_general(w, sh, dims, preferred_element_type=f32)
            if count % LANES:
                fill = jnp.zeros((prod.shape[0], LANES - count % LANES), f32)
                prod = jnp.concatenate([prod, fill], axis=1)
            for m in range(prod.shape[1] // LANES):
                for n, d in enumerate(blocks):
                    slab = prod[n * 64 : (n + 1) * 64, m * LANES : (m + 1) * LANES]
                    rows = pl.ds(d * 64, 64)
                    acc[lo + m, rows, :] = slab if fresh else acc[lo + m, rows, :] + slab
            fresh = False

    def finish(blocks):
        for i, (lo, count) in enumerate(CHUNKS):
            cross(0, acc0, blocks, lo, count)
            cross(1, acc1, blocks, lo, count)
            slabs = (count + LANES - 1) // LANES
            for d in blocks:
                for m in range(lo, lo + slabs):
                    val = (
                        acc0[m, pl.ds(d * 64, 32, stride=2), :]
                        + acc1[m, pl.ds(d * 64 + 1, 32, stride=2), :]
                    )
                    if d == 0:
                        rbuf[zh, m] = val
                    else:
                        ebuf[d - 1, m] = val
                if d:
                    at = pl.ds(lo, slabs)
                    send(
                        ebuf.at[d - 1, at], rbuf.at[zh, at],
                        esend.at[d - 1, i], erecv.at[d - 1, i], ep[d - 1],
                    )

    z_step(4)
    finish((1, 3, 0))
    for g in range(NX):
        arrive(unit_a(1 - core, z_origin(4, 0), g), hsend.at[g], hrecv.at[g], partner)
    finish((2,))

    left = lax.broadcasted_iota(jnp.int32, (32, LANES), 1) < NJ

    def turned(m):
        for slab in range(NS):
            val = rbuf[m, slab]
            swapped = pltpu.roll(val, NJ, 1)
            yield pltpu.roll(jnp.where(left, val, swapped), PJ * y, 1)
            yield pltpu.roll(jnp.where(left, swapped, val), PJ * y, 1)

    for d in (1, 3, 2):
        for i, (lo, count) in enumerate(CHUNKS):
            block = rbuf.at[rem(zh + NZH - d, NZH), pl.ds(lo, (count + LANES - 1) // LANES)]
            arrive(block, esend.at[d - 1, i], erecv.at[d - 1, i], ep[d - 1])
    for m in range(0, NZH, 2):
        for t, low, high in zip(range(NT), turned(m), turned(m + 1)):
            out[t, :, pl.ds(m * NJ, LANES)] = jnp.where(left, low, high)
    for c in started:
        c.wait_send()


def per_device(
    particles,
    ctf_class,
    orient_prior,
    ctf_curves,
    noise_weight,
    shift_phase,
    trans_index,
    projections,
    orient_subset,
):
    f32, bf16 = jnp.float32, jnp.bfloat16
    k = ctf_curves.shape[1]
    fill = (MAIN + 1) * LANES - k
    pc = jnp.concatenate([projections[:, 0, :], projections[:, 1, :]], axis=0)
    pc = jnp.pad(pc, ((0, 0), (0, fill)))

    dma = pltpu.SemaphoreType.DMA
    vm = pl.BlockSpec(memory_space=pltpu.VMEM)
    sm = pl.BlockSpec(memory_space=pltpu.SMEM)
    scores = pl.pallas_call(
        kernel,
        out_shape=jax.ShapeDtypeStruct((NT, 32, NZH * NJ), f32),
        in_specs=[sm] * 3 + [vm] * 6,
        out_specs=vm,
        scratch_shapes=[
            pltpu.VMEM((NY, 2 * PJ, KE), bf16),
            pltpu.VMEM((2, 4, KH), bf16),
            pltpu.VMEM((4, KH), bf16),
            pltpu.VMEM((2, NZH, NX, NZL, 8, KH), bf16),
            pltpu.VMEM((NT, KE), f32),
            pltpu.VMEM((NT, KE), f32),
            pltpu.VMEM((2, NT * NJ, KE), bf16),
            pltpu.VMEM((NS, ROWS, LANES), f32),
            pltpu.VMEM((NS, ROWS, LANES), f32),
            pltpu.VMEM((3, NS, 32, LANES), f32),
            pltpu.VMEM((NZH, NS, 32, LANES), f32),
            dma,
            dma((2, 4, NQ)),
            dma((2, 4, NQ)),
            dma((2, 4, NX)),
            dma((2, 4, NX)),
            dma((3,)),
            dma((3,)),
            dma((2, 4)),
            dma((2, 4)),
            dma((NX,)),
            dma((NX,)),
            dma,
            dma,
            dma((3, len(CHUNKS))),
            dma((3, len(CHUNKS))),
        ],
        compiler_params=pltpu.CompilerParams(
            collective_id=0, has_side_effects=True, vmem_limit_bytes=48 << 20
        ),
        name="scores",
    )(
        ctf_class, trans_index, orient_subset,
        pc, particles, orient_prior, ctf_curves, noise_weight[None, :], shift_phase,
    )
    return jnp.transpose(scores, (1, 0, 2))


def solution(mesh):
    placed = (
        P(("blk", "grp"), None, None),
        P(("blk", "grp")),
        P(("blk", "grp"), None),
        P(),
        P(),
        P(),
        P(),
        P(("grp", "blk"), None, None),
        P(("grp", "blk")),
    )
    return jax.shard_map(
        per_device, mesh=mesh, in_specs=placed, out_specs=P("blk", None, "grp"), check_vma=False
    )
```
